512 devices in a mesh: section: 16 (over z), expert: 32 (over x, y, core).
Axes of the slice: x: 4, y: 4, z: 16, core: 2. Of those that a mesh axis runs over, the one named last changes fastest.
Arguments:
- section_in: bfloat16 [16, 1024, 2048], P('section', 'expert'), may hold values from -6 to 6
- new_batch: bfloat16 [1, 1024, 2048], P(None, 'expert'), may hold values from -6 to 6
- stashed: bfloat16 [2, 16, 1024, 2048], P(None, 'section', 'expert'), may hold values from -6 to 6
- grad_in: bfloat16 [16, 1024, 2048], P('section', 'expert'), may hold values from -6 to 6
- loss_grad: bfloat16 [1, 1024, 2048], P(None, 'expert'), may hold values from -6 to 6
- routes: int32 [2, 2, 16, 1024, 2], P(None, None, 'section', 'expert'), may hold values from 0 to 7, all different within a row; in each aligned block of 32 rows (0 to 31, 32 to 63, ..., all dimensions but the last counted through in order) at most 8 rows name the same one
- counts: int32 [2, 2, 16, 1024], P(None, None, 'section', 'expert'), may hold values from 0 to 2, as said below
- norm_gain: float32 [16, 2048], P('section'), may hold values from 0.1 to 1.9
- w_router: bfloat16 [16, 2048, 8], P('section'), may hold values from -0.125 to 0.125
- w_gate: bfloat16 [16, 2048, 8192], P('section', None, 'expert'), may hold values from -0.125 to 0.125
- w_up: bfloat16 [16, 2048, 8192], P('section', None, 'expert'), may hold values from -0.125 to 0.125
- w_down: bfloat16 [16, 8192, 2048], P('section', 'expert'), may hold values from -0.1875 to 0.1875
- lam: float32 [16], P('section'), may hold values from 4 to 40
Outputs:
- fwd_out: bfloat16 [2, 16, 1024, 2048], P(None, 'section', 'expert')
- grad_out: bfloat16 [2, 16, 1024, 2048], P(None, 'section', 'expert')
- lam_out: float32 [16], P('section')
The draws below stay inside these ranges and needn't reach their ends.
Inputs may be any that keep to these rules, and one draw needn't show every extreme that they name: routes[m, k, s, t] names 2 different experts; among the 32 tokens of one device's aligned block no expert is named more than 8 times. counts[m, k, s, t] active entries come first in the token's list.
All inputs are finite; a program needn't handle non-finite values.
Results may differ from the reference program's by a relative error of at most 0.01.
Values may be sent and summed in bfloat16 or wider, within the bound.
A program may use at most 128 MiB of HBM per device.

```python
import math
import jax
import jax.numpy as jnp
import numpy as np
from jax import lax

D = 2048
FF = 1024
SPLIT = 4
TICKS = 2
TOK_DEV = 32
FF_DEV = 256
EXPERTS = 8
TOP = 2
CAP = 8
SECTIONS = 16
MB_TOK = 1024
N_EXPERT = 32


def draw_counts(key, part):
    position = jnp.arange(MB_TOK, dtype=jnp.int32)
    ceiling = 2 + 6 * position // MB_TOK
    drawn = jax.random.randint(key, (2, TICKS, SECTIONS, MB_TOK), 0, ceiling)
    return jnp.minimum(drawn, TOP).astype(jnp.int32)


def level_of(rng, dims, shards, low, largest):
    def one(axis_at, blocks):
        draws = jax.random.uniform(jax.random.fold_in(jax.random.fold_in(rng, 6), axis_at), (blocks,), jnp.float32, low / len(shards), largest / len(shards))
        return jnp.repeat(jnp.exp(draws), dims[axis_at] // blocks).reshape((-1,) + (1,) * (len(dims) - axis_at - 1))

    level = one(*shards[0])
    for cut in shards[1:]:
        level = level * one(*cut)
    return level


def routed_block(stream_key, own, number, rows, count, top, reach, skew):
    sequence = jax.random.permutation(stream_key, count)
    crowded, common = shares(count, rows * top, reach, skew, True), shares(count, rows * top, reach, skew, False)
    places = jnp.arange(count)

    def named(tallies, turn):
        used = int((tallies > 0).sum())
        fixed = max(1, used // 4)
        moved = fixed + (places - fixed + turn * (used - fixed)) % max(1, count - fixed)
        return jnp.zeros((count,), jnp.int32).at[sequence[jnp.where(places < fixed, places, moved)]].set(jnp.asarray(tallies, jnp.int32))

    tallies = jnp.where(number % 4 == 0, named(crowded, number // 4), named(common, number - number // 4 - 1))
    mixed = jax.random.permutation(jax.random.fold_in(own, 3), count)
    source_of, sink = mixed[0:count // 2 * 2:2], mixed[1:count // 2 * 2:2]
    room = jnp.minimum(tallies[source_of] - 1, reach - tallies[sink]) // 2
    room = jnp.where((source_of == sequence[0]) | (sink == sequence[0]) | (tallies[sink] == 0), 0, jnp.maximum(room, 0))
    moved = jax.random.randint(jax.random.fold_in(own, 4), (count // 2,), 0, 1 << 20) % (room + 1)
    tallies = tallies.at[source_of].add(-moved).at[sink].add(moved)
    items = jnp.searchsorted(jnp.cumsum(tallies), jnp.arange(rows * top), side="right").astype(jnp.int32)
    listing = items.reshape(top, rows).T
    listing = listing[jax.random.permutation(jax.random.fold_in(own, 1), rows)]
    turn = jax.random.randint(jax.random.fold_in(own, 2), (rows, 1), 0, top)
    return jnp.take_along_axis(listing, (jnp.arange(top)[None, :] + turn) % top, axis=1)


def shares(number_of, total, reach, skew, full):
    loads = [(1 << 20) // math.isqrt(standing ** skew) + 1 for standing in range(1, number_of + 1)]
    largest = reach if full else min(reach, max(-(-total // number_of), total * loads[0] // sum(loads)))
    least = 1 if total - largest >= number_of - 1 else 0
    given, surplus = [largest] + [least] * (number_of - 1), total - largest - least * (number_of - 1)
    while surplus > 0:
        candidates = [i for i in range(1, number_of) if given[i] < largest] or [i for i in range(1, number_of) if given[i] < reach]
        mass, left = sum([loads[i] for i in candidates]), surplus
        for i in candidates:
            addition = min(reach - given[i], max(1, left * loads[i] // mass), surplus)
            given[i] = given[i] + addition
            surplus = surplus - addition
    return np.array(given)


def noise(rng, dims, deviation, reach, cuts=(), kind=jnp.bfloat16):
    values = jax.random.normal(rng, dims, jnp.float32) * deviation
    if len(cuts) > 0:
        values = level_of(rng, dims, cuts, -0.22, 0.18) * values
    return jnp.clip(values, min=-reach, max=reach).astype(kind)


def setup_inputs(seed: int = 0) -> dict:
    streams_of = jax.random.split(jax.random.key(seed), 14)
    section_in = noise(streams_of[0], (SECTIONS, MB_TOK, D), 1.0, 6.0, ((0, 16), (1, 32)))
    new_batch = noise(streams_of[1], (TICKS - 1, MB_TOK, D), 1.0, 6.0, ((1, 32),))
    stashed = noise(streams_of[2], (TICKS, SECTIONS, MB_TOK, D), 1.0, 6.0, ((1, 16), (2, 32)))
    grad_in = noise(streams_of[3], (SECTIONS, MB_TOK, D), 1.0, 6.0, ((0, 16), (1, 32)))
    loss_grad = noise(streams_of[4], (TICKS - 1, MB_TOK, D), 1.0, 6.0, ((1, 32),))
    routes_keys = jax.random.split(jax.random.fold_in(streams_of[5], 1), 2 * TICKS * SECTIONS * MB_TOK // TOK_DEV)
    routes_turns = jax.random.permutation(jax.random.fold_in(streams_of[5], 3), 2 * TICKS * SECTIONS * MB_TOK // TOK_DEV)
    routes = jax.vmap(lambda own, number: routed_block(jax.random.fold_in(streams_of[5], 2), own, number, TOK_DEV, EXPERTS, TOP, CAP, 2))(routes_keys, routes_turns).reshape((2, TICKS, SECTIONS, MB_TOK, TOP))
    counts = draw_counts(jax.random.fold_in(streams_of[13], 71), 0)
    norm_gain = jnp.clip(1.0 + 0.18 * jax.random.normal(streams_of[7], (SECTIONS, D), jnp.float32), 0.1, 1.9)
    w_router = noise(streams_of[8], (SECTIONS, D, EXPERTS), D ** -0.5, 0.125, ((0, 16),))
    w_gate = noise(streams_of[9], (SECTIONS, D, EXPERTS * FF), D ** -0.5, 0.125, ((0, 16), (2, 32)))
    w_up = noise(streams_of[10], (SECTIONS, D, EXPERTS * FF), D ** -0.5, 0.125, ((0, 16), (2, 32)))
    w_down = noise(streams_of[11], (SECTIONS, EXPERTS * FF, D), FF ** -0.5, 0.1875, ((0, 16), (1, 32)))
    lam = jnp.clip(jnp.exp(math.log(40.0) - 2.3025851 * jax.random.uniform(streams_of[12], (SECTIONS,), jnp.float32) ** level_of(streams_of[12], (SECTIONS,), ((0, 16),), -0.2, 0.2)), 4.0, 40.0)
    return dict(section_in=section_in, new_batch=new_batch, stashed=stashed, grad_in=grad_in, loss_grad=loss_grad, routes=routes, counts=counts, norm_gain=norm_gain, w_router=w_router, w_gate=w_gate, w_up=w_up, w_down=w_down, lam=lam)


def norm_rows(values, gain_row):
    return values * lax.rsqrt(lax.optimization_barrier(jnp.mean(values * values, axis=-1, keepdims=True)) + 1e-05) * gain_row

def quarter_work(rows_f, rows_b, grads, scales, gate_q, up_q, down_q):
    all_rows = jnp.concatenate([rows_f, rows_b], axis=0)
    pre_gate = jnp.dot(all_rows, gate_q, preferred_element_type=jnp.float32)
    pre_up = jnp.dot(all_rows, up_q, preferred_element_type=jnp.float32)
    activated = jax.nn.silu(pre_gate)
    hidden = (activated * pre_up).astype(jnp.bfloat16)
    projected = jnp.dot(hidden, down_q, preferred_element_type=jnp.float32).astype(jnp.bfloat16)
    half_rows = rows_f.shape[0]
    scaled = (scales.astype(jnp.float32)[:, None] * grads.astype(jnp.float32)).astype(jnp.bfloat16)
    back_h = jnp.dot(scaled, down_q.T, preferred_element_type=jnp.float32)
    gate_tail = pre_gate[half_rows:]
    sigmoid_g = jax.nn.sigmoid(gate_tail)
    silu_slope = sigmoid_g * (1.0 + gate_tail * (1.0 - sigmoid_g))
    d_gate = (back_h * pre_up[half_rows:] * silu_slope).astype(jnp.bfloat16)
    d_up = (back_h * activated[half_rows:]).astype(jnp.bfloat16)
    d_rows = (jnp.dot(d_gate, gate_q.T, preferred_element_type=jnp.float32) + jnp.dot(d_up, up_q.T, preferred_element_type=jnp.float32)).astype(jnp.bfloat16)
    inner_dot = lax.optimization_barrier(jnp.sum(grads.astype(jnp.float32) * projected[half_rows:].astype(jnp.float32), axis=-1)).astype(jnp.bfloat16)
    return (projected[:half_rows], d_rows, inner_dot)

def slot_place(route):
    blocks = route.reshape(N_EXPERT, TOK_DEV * TOP)
    onehot = (blocks[:, :, None] == jnp.arange(EXPERTS, dtype=jnp.int32)[None, None, :]).astype(jnp.int32)
    slot_rank = lax.optimization_barrier(jnp.sum((jnp.cumsum(onehot, axis=1) - 1) * onehot, axis=2))
    source = jnp.arange(N_EXPERT, dtype=jnp.int32)[:, None]
    return (source * CAP + slot_rank).reshape(MB_TOK, TOP).astype(jnp.int32)

def expert_step(item):
    rows_f, rows_b, grads, scales, gate_e, up_e, down_e = item
    total_y = jnp.zeros(rows_f.shape, jnp.float32)
    total_dn = jnp.zeros(rows_f.shape, jnp.float32)
    total_dot = jnp.zeros(rows_f.shape[:1], jnp.float32)
    for quarter_idx in range(SPLIT):
        projected, d_rows, inner_dot = quarter_work(rows_f, rows_b, grads, scales, gate_e[quarter_idx], up_e[quarter_idx], down_e[quarter_idx])
        total_y = total_y + projected.astype(jnp.float32)
        total_dn = total_dn + d_rows.astype(jnp.float32)
        total_dot = total_dot + inner_dot.astype(jnp.float32)
    return (total_y, total_dn, total_dot)

def section_step(item):
    forward_x, stash_x, cotangent, route_f, count_f, route_b, count_b, gain_row, router, gate_cols, up_cols, down_rows, weight = item
    slots = jnp.arange(TOP, dtype=jnp.int32)[None, :]
    live_f = (slots < count_f[:, None]).astype(jnp.float32)
    live_b = (slots < count_b[:, None]).astype(jnp.float32)
    normed_f = norm_rows(forward_x.astype(jnp.float32), gain_row).astype(jnp.bfloat16)
    picked_f = jnp.take_along_axis(jnp.dot(normed_f, router, preferred_element_type=jnp.float32), route_f, axis=1)
    gate_f = jax.nn.softplus(picked_f) * live_f
    normed_raw, pullback = jax.vjp(lambda values: norm_rows(values, gain_row), stash_x.astype(jnp.float32))
    normed_b = normed_raw.astype(jnp.bfloat16)
    picked_b = jnp.take_along_axis(jnp.dot(normed_b, router, preferred_element_type=jnp.float32), route_b, axis=1)
    gate_b = jax.nn.softplus(picked_b) * live_b
    place_f = slot_place(route_f)
    place_b = slot_place(route_b)
    drop_f = jnp.where(live_f > 0, route_f, EXPERTS).astype(jnp.int32)
    drop_b = jnp.where(live_b > 0, route_b, EXPERTS).astype(jnp.int32)
    buffer_shape = (EXPERTS, N_EXPERT * CAP, D)
    spread_shape = (MB_TOK, TOP, D)
    buffer_f = jnp.zeros(buffer_shape, jnp.bfloat16).at[drop_f, place_f].set(jnp.broadcast_to(normed_f[:, None, :], spread_shape), mode='drop')
    buffer_b = jnp.zeros(buffer_shape, jnp.bfloat16).at[drop_b, place_b].set(jnp.broadcast_to(normed_b[:, None, :], spread_shape), mode='drop')
    buffer_d = jnp.zeros(buffer_shape, jnp.bfloat16).at[drop_b, place_b].set(jnp.broadcast_to(cotangent[:, None, :], spread_shape), mode='drop')
    buffer_s = jnp.zeros((EXPERTS, N_EXPERT * CAP), jnp.float32).at[drop_b, place_b].set(gate_b, mode='drop').astype(jnp.bfloat16)
    gate_four = jnp.transpose(gate_cols.reshape(D, EXPERTS, SPLIT, FF_DEV), (1, 2, 0, 3))
    up_four = jnp.transpose(up_cols.reshape(D, EXPERTS, SPLIT, FF_DEV), (1, 2, 0, 3))
    down_four = down_rows.reshape(EXPERTS, SPLIT, FF_DEV, D)
    y_all, dn_all, dot_all = lax.map(expert_step, (buffer_f, buffer_b, buffer_d, buffer_s, gate_four, up_four, down_four))
    y_tok = y_all[route_f, place_f]
    out_f = (forward_x.astype(jnp.float32) + lax.optimization_barrier(jnp.sum(gate_f[:, :, None] * y_tok, axis=1))).astype(jnp.bfloat16)
    dpick = (dot_all[route_b, place_b] + weight) * jax.nn.sigmoid(picked_b) * live_b
    onehot_b = (route_b[:, :, None] == jnp.arange(EXPERTS, dtype=jnp.int32)[None, None, :]).astype(jnp.float32)
    dlogit = lax.optimization_barrier(jnp.sum(onehot_b * dpick[:, :, None], axis=1))
    dnorm = lax.optimization_barrier(jnp.sum(live_b[:, :, None] * dn_all[route_b, place_b], axis=1)) + jnp.dot(dlogit, router.astype(jnp.float32).T, precision=lax.Precision.HIGHEST)
    grad_x = (cotangent.astype(jnp.float32) + pullback(dnorm)[0]).astype(jnp.bfloat16)
    return (out_f, grad_x)

def reference(section_in, new_batch, stashed, grad_in, loss_grad, routes, counts, norm_gain, w_router, w_gate, w_up, w_down, lam):
    totals = lax.optimization_barrier(jnp.sum(counts[0], axis=-1)).astype(jnp.float32)
    weight = lam
    forward_x = section_in
    cotangent = grad_in
    fwd_list = []
    grad_list = []
    for tick_num in range(TICKS):
        if tick_num > 0:
            forward_x = jnp.concatenate([new_batch[tick_num - 1][None], fwd_list[-1][:-1]], axis=0)
            cotangent = jnp.concatenate([grad_list[-1][1:], loss_grad[tick_num - 1][None]], axis=0)
        out_f, grad_x = lax.map(section_step, (forward_x, stashed[tick_num], cotangent, routes[0, tick_num], counts[0, tick_num], routes[1, tick_num], counts[1, tick_num], norm_gain, w_router, w_gate, w_up, w_down, weight))
        fwd_list.append(out_f)
        grad_list.append(grad_x)
        weight = weight * jnp.exp(4.0 * (totals[tick_num] / (MB_TOK * TOP) - 0.5))
    return (jnp.stack(fwd_list), jnp.stack(grad_list), weight)
```

```python
import jax
import jax.numpy as jnp
from jax import lax
from jax.sharding import PartitionSpec as P

SPLIT = 4
TICKS = 2
LANES = 128


def from_behind(block, axis, distance):
    devices = range(lax.axis_size(axis))
    route = [(i - distance, i) for i in devices if i - distance in devices]
    return lax.ppermute(block, axis, route)


def expert_work(rows, carried, gate_q, up_q, down_q, capacity):
    sources, pair_rows, width = rows.shape
    hidden_q = gate_q.shape[1]
    flat = rows.reshape(sources * pair_rows, width)
    pre_gate = jnp.dot(flat, gate_q, preferred_element_type=jnp.float32)
    pre_up = jnp.dot(flat, up_q, preferred_element_type=jnp.float32)
    sigmoid_g = jax.nn.sigmoid(pre_gate)
    activated = pre_gate * sigmoid_g
    hidden = (activated * pre_up).astype(jnp.bfloat16)

    def half(value, which):
        paired = value.reshape(sources, 2, capacity, hidden_q)
        return paired[:, which].reshape(sources * capacity, hidden_q)

    y_part = jnp.dot(half(hidden, 0), down_q, preferred_element_type=jnp.float32)
    grads = carried[:, :, :width].reshape(sources * capacity, width)
    scales = carried[:, :, width].reshape(sources * capacity, 1).astype(jnp.float32)
    plain_h = jnp.dot(grads, down_q.T, preferred_element_type=jnp.float32)
    inner_dot = jnp.sum(plain_h * half(hidden, 1).astype(jnp.float32), axis=-1, keepdims=True)
    back_h = plain_h * scales
    slope_g = half(sigmoid_g, 1)
    d_gate = back_h * half(pre_up, 1) * slope_g * (1.0 + half(pre_gate, 1) * (1.0 - slope_g))
    d_up = back_h * half(activated, 1)
    dn_part = jnp.dot(
        d_gate.astype(jnp.bfloat16), gate_q.T, preferred_element_type=jnp.float32
    ) + jnp.dot(d_up.astype(jnp.bfloat16), up_q.T, preferred_element_type=jnp.float32)
    dots = jnp.broadcast_to(inner_dot, (sources * capacity, LANES))
    joined = jnp.concatenate([y_part, dn_part, dots], axis=-1).astype(jnp.bfloat16)
    return joined.reshape(sources, capacity, 2 * width + LANES)


def spread(block, experts):
    repeated = jnp.broadcast_to(block[:, None], (experts, SPLIT) + block.shape[1:])
    return repeated.reshape((experts * SPLIT,) + block.shape[1:])


def on_device(
    section_in,
    new_batch,
    stashed,
    grad_in,
    loss_grad,
    routes,
    counts,
    norm_gain,
    w_router,
    w_gate,
    w_up,
    w_down,
    lam,
):
    f32, bf16 = jnp.float32, jnp.bfloat16
    section_pos = lax.axis_index("section")
    last_section = lax.axis_size("section") - 1
    tok_rows, width = section_in.shape[1:]
    top_slots = routes.shape[-1]
    experts = w_router.shape[-1]
    capacity = SPLIT * min(
        tok_rows // (2 * SPLIT), 5 * tok_rows * top_slots // (4 * experts * SPLIT)
    )
    slots = experts * capacity
    entries = tok_rows * top_slots
    share_total = tok_rows * lax.axis_size("expert") * top_slots
    gain_row = norm_gain[0]
    router = w_router[0]
    router_t = router.astype(f32).T
    gate_cols, up_cols, down_rows = w_gate[0], w_up[0], w_down[0]
    route = routes[:, :, 0]
    count = counts[:, :, 0]
    flat = route.reshape(2, TICKS, entries)
    earlier = jnp.arange(entries)[None, :] < jnp.arange(entries)[:, None]
    rank = jnp.sum(
        ((flat[..., :, None] == flat[..., None, :]) & earlier).astype(jnp.int32), axis=-1
    )
    target = (flat * capacity + rank).reshape(2, TICKS, tok_rows, top_slots)
    live = jnp.arange(top_slots, dtype=jnp.int32) < count[..., None]
    table = ((target[..., None] == jnp.arange(slots)) & live[..., None]).astype(f32)
    chosen = (route[..., None] == jnp.arange(experts)).astype(f32)
    dispatch = jnp.sum(table, axis=3).astype(bf16)
    live = live.astype(f32)
    own_totals = jnp.sum(count[0], axis=-1).astype(f32)

    def norm_of(values):
        values = values.astype(f32)
        inverse = lax.rsqrt(jnp.mean(values * values, axis=-1, keepdims=True) + 1e-05)
        return values * inverse, inverse

    def picked_of(normed, m, k):
        logits = jnp.dot(normed, router, preferred_element_type=f32)
        return jnp.sum(chosen[m, k] * logits[:, None, :], axis=-1)

    def placed(m, k, rows):
        return lax.dot_general(
            dispatch[m, k], rows, (((0,), (0,)), ((), ())), preferred_element_type=f32
        ).astype(bf16)

    backs = []
    for k in range(TICKS):
        unit, inverse = norm_of(stashed[k, 0])
        normed = (unit * gain_row).astype(bf16)
        picked = picked_of(normed, 1, k)
        gate = jax.nn.softplus(picked) * live[1, k]
        scale = jnp.sum(table[1, k] * gate[:, :, None], axis=(0, 1))
        backs.append((unit, inverse, placed(1, k, normed), picked, scale))

    weight = lam[0]
    forward_x = section_in[0]
    cotangent = grad_in[0]
    fwd_list = []
    grad_list = []
    totals = None
    for k in range(TICKS):
        if k > 0:
            arriving = from_behind(fwd_list[-1], "section", 1)
            forward_x = jnp.where(section_pos == 0, new_batch[k - 1], arriving)
            coming = from_behind(grad_list[-1], "section", -1)
            cotangent = jnp.where(section_pos == last_section, loss_grad[k - 1], coming)
        unit_b, inverse_b, rows_b, picked_b, scale_b = backs[k]
        unit_f, _ = norm_of(forward_x)
        normed_f = (unit_f * gain_row).astype(bf16)
        gate_f = jax.nn.softplus(picked_of(normed_f, 0, k)) * live[0, k]
        rows = jnp.concatenate(
            [
                placed(0, k, normed_f).reshape(experts, capacity, width),
                rows_b.reshape(experts, capacity, width),
            ],
            axis=1,
        )
        lane = jnp.arange(LANES)
        extra = jnp.where(
            lane == 0,
            scale_b[:, None],
            jnp.where(lane == 1, own_totals[0], jnp.where(lane == 2, own_totals[1], 0.0)),
        ).astype(bf16)
        carried = jnp.concatenate([placed(1, k, cotangent), extra], axis=1)
        carried = carried.reshape(experts, capacity, width + LANES)
        got_rows = lax.all_to_all(spread(rows, experts), "expert", 0, 0, tiled=True)
        got_carried = lax.all_to_all(spread(carried, experts), "expert", 0, 0, tiled=True)
        if totals is None:
            seen = got_carried[:, 0, width + 1 : width + 1 + TICKS].astype(f32)
            totals = jnp.sum(seen, axis=0)
        partial = expert_work(got_rows, got_carried, gate_cols, up_cols, down_rows, capacity)
        back = lax.all_to_all(partial, "expert", 0, 0, tiled=True)
        summed = jnp.sum(
            back.astype(f32).reshape(experts, SPLIT, capacity, 2 * width + LANES), axis=1
        ).reshape(slots, 2 * width + LANES)
        combine_f = jnp.sum(table[0, k] * gate_f[:, :, None], axis=1)
        out_f = forward_x.astype(f32) + jnp.dot(
            combine_f, summed[:, :width], precision=lax.Precision.HIGHEST
        )
        dots = jnp.sum(table[1, k] * summed[:, 2 * width], axis=-1)
        dpick = (dots + weight) * jax.nn.sigmoid(picked_b) * live[1, k]
        dlogit = jnp.sum(chosen[1, k] * dpick[:, :, None], axis=1)
        dnorm = jnp.dot(
            jnp.sum(table[1, k], axis=1),
            summed[:, width : 2 * width],
            precision=lax.Precision.HIGHEST,
        ) + jnp.dot(dlogit, router_t, precision=lax.Precision.HIGHEST)
        scaled = dnorm * gain_row
        along = jnp.mean(scaled * unit_b, axis=-1, keepdims=True)
        grad_x = cotangent.astype(f32) + inverse_b * (scaled - unit_b * along)
        fwd_list.append(out_f.astype(bf16))
        grad_list.append(grad_x.astype(bf16))
        weight = weight * jnp.exp(4.0 * (totals[k] / share_total - 0.5))
    return (jnp.stack(fwd_list)[:, None], jnp.stack(grad_list)[:, None], weight.reshape(1))


def solution(mesh):
    in_specs = (
        P("section", "expert", None),
        P(None, "expert", None),
        P(None, "section", "expert", None),
        P("section", "expert", None),
        P(None, "expert", None),
        P(None, None, "section", "expert", None),
        P(None, None, "section", "expert"),
        P("section", None),
        P("section", None, None),
        P("section", None, "expert"),
        P("section", None, "expert"),
        P("section", "expert", None),
        P("section"),
    )
    out_specs = (
        P(None, "section", "expert", None),
        P(None, "section", "expert", None),
        P("section"),
    )
    return jax.shard_map(
        on_device, mesh=mesh, in_specs=in_specs, out_specs=out_specs, check_vma=False
    )
```

```python
import functools

import jax
import jax.numpy as jnp
from jax import lax
from jax.experimental import pallas as pl
from jax.experimental.pallas import tpu as pltpu
from jax.sharding import PartitionSpec as P

SPLIT = 4
TICKS = 2
LANES = 128


def from_behind(block, axis, distance):
    devices = range(lax.axis_size(axis))
    route = [(i - distance, i) for i in devices if i - distance in devices]
    return lax.ppermute(block, axis, route)


MESH = pl.DeviceIdType.MESH
SIDE = 4
CHIPS = SIDE * SIDE


class Place:
    def __init__(self):
        self.section = lax.axis_index("section")
        me = lax.axis_index("expert")
        self.chip = me // 2
        self.core = me % 2

    def away(self, step, sign):
        x = (self.chip // SIDE + sign * (step // SIDE) + SIDE) % SIDE
        y = (self.chip % SIDE + sign * (step % SIDE) + SIDE) % SIDE
        return x * SIDE + y

    def same_core(self, chip):
        return (self.section, chip * 2 + self.core)

    def other_core(self):
        return (self.section, self.chip * 2 + 1 - self.core)

    def greet(self):
        barrier = pltpu.get_barrier_semaphore()

        def signal(step, carry):
            pl.semaphore_signal(
                barrier,
                inc=1,
                device_id=self.same_core(self.away(step, 1)),
                device_id_type=MESH,
            )
            return carry

        lax.fori_loop(1, CHIPS, signal, 0)
        pl.semaphore_signal(
            barrier, inc=1, device_id=self.other_core(), device_id_type=MESH
        )
        pl.semaphore_wait(barrier, CHIPS)


def steps_of(first, body):
    def step_once(step, carry):
        body(step)
        return carry

    lax.fori_loop(first, CHIPS, step_once, 0)


def remote(src, dst, send, recv, device):
    return pltpu.make_async_remote_copy(
        src_ref=src,
        dst_ref=dst,
        send_sem=send,
        recv_sem=recv,
        device_id=device,
        device_id_type=MESH,
    )


def dispatch_kernel(number, *refs):
    sources, results = refs[:number], refs[number : 2 * number]
    send, recv, pass_send, pass_recv, own = refs[2 * number :]
    at = Place()
    at.greet()
    streams = range(number)

    def outward(i, step):
        goal = at.away(step, 1)
        return remote(
            sources[i].at[goal // 2],
            results[i].at[at.core * CHIPS + at.chip],
            send.at[i, step],
            recv.at[i, step],
            at.same_core(goal),
        )

    def passed(i, step):
        slot = at.core * CHIPS + at.away(step, -1)
        return remote(
            results[i].at[slot],
            results[i].at[slot],
            pass_send.at[i, step],
            pass_recv.at[i, step],
            at.other_core(),
        )

    def own_copy(i):
        return pltpu.make_async_copy(
            sources[i].at[at.chip // 2], results[i].at[at.core * CHIPS + at.chip], own.at[i]
        )

    def start(step):
        for i in streams:
            outward(i, step).start()

    def hand_over(step):
        for i in streams:
            outward(i, step).wait_recv()
            passed(i, step).start()

    def finish(step):
        for i in streams:
            passed(i, step).wait_send()
            passed(i, step).wait_recv()

    def sent(step):
        for i in streams:
            outward(i, step).wait_send()

    for i in streams:
        own_copy(i).start()
    steps_of(1, start)
    for i in streams:
        own_copy(i).wait()
        passed(i, 0).start()
    steps_of(1, hand_over)
    steps_of(1, sent)
    steps_of(0, finish)


def collect_kernel(number, *refs):
    parts, results = refs[:number], refs[number : 2 * number]
    arrived, joined = refs[2 * number : 3 * number], refs[3 * number : 4 * number]
    send, recv, pass_send, pass_recv = refs[4 * number :]
    at = Place()
    at.greet()
    streams = range(number)

    def passed(i, step):
        goal = at.away(step, 1)
        return remote(
            parts[i].at[(1 - at.core) * CHIPS + goal],
            arrived[i].at[goal],
            pass_send.at[i, step],
            pass_recv.at[i, step],
            at.other_core(),
        )

    def outward(i, step):
        goal = at.away(step, 1)
        return remote(
            joined[i].at[goal],
            results[i].at[at.chip],
            send.at[i, step],
            recv.at[i, step],
            at.same_core(goal),
        )

    def added(i, step):
        passed(i, step).wait_recv()
        goal = at.away(step, 1)
        total = parts[i][at.core * CHIPS + goal].astype(jnp.float32) + arrived[i][goal].astype(
            jnp.float32
        )
        return goal, total.astype(jnp.bfloat16)

    def start(step):
        for i in streams:
            passed(i, step).start()

    def send_on(step):
        for i in streams:
            goal, total = added(i, step)
            joined[i][goal] = total
            outward(i, step).start()

    def finish(step):
        for i in streams:
            outward(i, step).wait_send()
            outward(i, step).wait_recv()

    def sent(step):
        for i in streams:
            passed(i, step).wait_send()

    steps_of(1, start)
    for i in streams:
        passed(i, 0).start()
    steps_of(1, send_on)
    for i in streams:
        goal, total = added(i, 0)
        results[i][goal] = total
    steps_of(0, sent)
    steps_of(1, finish)


def dispatch_rows(arrays):
    number = len(arrays)
    whole = pl.BlockSpec(memory_space=pltpu.VMEM)
    sems = pltpu.SemaphoreType.DMA
    return pl.pallas_call(
        functools.partial(dispatch_kernel, number),
        out_shape=[jax.ShapeDtypeStruct((2 * CHIPS,) + a.shape[1:], a.dtype) for a in arrays],
        in_specs=[whole] * number,
        out_specs=[whole] * number,
        scratch_shapes=[sems((number, CHIPS))] * 4 + [sems((number,))],
        compiler_params=pltpu.CompilerParams(
            collective_id=0, has_side_effects=True, vmem_limit_bytes=32 * 2**20
        ),
        name="dispatch_rows",
    )(*arrays)


def collect_rows(arrays):
    number = len(arrays)
    whole = pl.BlockSpec(memory_space=pltpu.VMEM)
    sems = pltpu.SemaphoreType.DMA
    blocks = [(CHIPS,) + a.shape[1:] for a in arrays]
    return pl.pallas_call(
        functools.partial(collect_kernel, number),
        out_shape=[jax.ShapeDtypeStruct(s, a.dtype) for s, a in zip(blocks, arrays)],
        in_specs=[whole] * number,
        out_specs=[whole] * number,
        scratch_shapes=[pltpu.VMEM(s, a.dtype) for s, a in zip(blocks, arrays)] * 2
        + [sems((number, CHIPS))] * 4,
        compiler_params=pltpu.CompilerParams(
            collective_id=1, has_side_effects=True, vmem_limit_bytes=32 * 2**20
        ),
        name="collect_rows",
    )(*arrays)


def expert_work(rows_f, rows_b, carried, gate_q, up_q, down_q):
    sources, capacity, width = rows_f.shape

    def first(rows):
        flat = rows.reshape(sources * capacity, width)
        pre_gate = jnp.dot(flat, gate_q, preferred_element_type=jnp.float32)
        pre_up = jnp.dot(flat, up_q, preferred_element_type=jnp.float32)
        sigmoid_g = jax.nn.sigmoid(pre_gate)
        activated = pre_gate * sigmoid_g
        hidden = (activated * pre_up).astype(jnp.bfloat16)
        return pre_gate, pre_up, sigmoid_g, activated, hidden

    hidden_f = first(rows_f)[-1]
    pre_gate, pre_up, sigmoid_g, activated, hidden_b = first(rows_b)
    y_part = jnp.dot(hidden_f, down_q, preferred_element_type=jnp.float32).astype(jnp.bfloat16)
    grads = carried[:, :, :width].reshape(sources * capacity, width)
    scales = carried[:, :, width].reshape(sources * capacity, 1).astype(jnp.float32)
    plain_h = jnp.dot(grads, down_q.T, preferred_element_type=jnp.float32)
    inner_dot = jnp.sum(plain_h * hidden_b.astype(jnp.float32), axis=-1, keepdims=True)
    back_h = plain_h * scales
    d_gate = back_h * pre_up * sigmoid_g * (1.0 + pre_gate * (1.0 - sigmoid_g))
    d_up = back_h * activated
    dn_part = jnp.dot(
        d_gate.astype(jnp.bfloat16), gate_q.T, preferred_element_type=jnp.float32
    ) + jnp.dot(d_up.astype(jnp.bfloat16), up_q.T, preferred_element_type=jnp.float32)
    dots = jnp.broadcast_to(inner_dot, (sources * capacity, LANES)).astype(jnp.bfloat16)
    shape = (sources, capacity)
    return (
        y_part.reshape(shape + (width,)),
        dn_part.astype(jnp.bfloat16).reshape(shape + (width,)),
        dots.reshape(shape + (LANES,)),
    )


def on_device(
    section_in,
    new_batch,
    stashed,
    grad_in,
    loss_grad,
    routes,
    counts,
    norm_gain,
    w_router,
    w_gate,
    w_up,
    w_down,
    lam,
):
    f32, bf16 = jnp.float32, jnp.bfloat16
    section_pos = lax.axis_index("section")
    last_section = lax.axis_size("section") - 1
    tok_rows, width = section_in.shape[1:]
    top_slots = routes.shape[-1]
    experts = w_router.shape[-1]
    capacity = SPLIT * min(
        tok_rows // (2 * SPLIT), 5 * tok_rows * top_slots // (4 * experts * SPLIT)
    )
    slots = experts * capacity
    entries = tok_rows * top_slots
    share_total = tok_rows * lax.axis_size("expert") * top_slots
    gain_row = norm_gain[0]
    router = w_router[0]
    router_t = router.astype(f32).T
    gate_cols, up_cols, down_rows = w_gate[0], w_up[0], w_down[0]
    route = routes[:, :, 0]
    count = counts[:, :, 0]
    flat = route.reshape(2, TICKS, entries)
    earlier = jnp.arange(entries)[None, :] < jnp.arange(entries)[:, None]
    rank = jnp.sum(
        ((flat[..., :, None] == flat[..., None, :]) & earlier).astype(jnp.int32), axis=-1
    )
    target = (flat * capacity + rank).reshape(2, TICKS, tok_rows, top_slots)
    live = jnp.arange(top_slots, dtype=jnp.int32) < count[..., None]
    table = ((target[..., None] == jnp.arange(slots)) & live[..., None]).astype(f32)
    chosen = (route[..., None] == jnp.arange(experts)).astype(f32)
    dispatch = jnp.sum(table, axis=3).astype(bf16)
    live = live.astype(f32)
    own_totals = jnp.sum(count[0], axis=-1).astype(f32)

    def norm_of(values):
        values = values.astype(f32)
        inverse = lax.rsqrt(jnp.mean(values * values, axis=-1, keepdims=True) + 1e-05)
        return values * inverse, inverse

    def picked_of(normed, m, k):
        logits = jnp.dot(normed, router, preferred_element_type=f32)
        return jnp.sum(chosen[m, k] * logits[:, None, :], axis=-1)

    def placed(m, k, rows):
        return lax.dot_general(
            dispatch[m, k], rows, (((0,), (0,)), ((), ())), preferred_element_type=f32
        ).astype(bf16)

    backs = []
    for k in range(TICKS):
        unit, inverse = norm_of(stashed[k, 0])
        normed = (unit * gain_row).astype(bf16)
        picked = picked_of(normed, 1, k)
        gate = jax.nn.softplus(picked) * live[1, k]
        scale = jnp.sum(table[1, k] * gate[:, :, None], axis=(0, 1))
        backs.append((unit, inverse, placed(1, k, normed), picked, scale))

    weight = lam[0]
    forward_x = section_in[0]
    cotangent = grad_in[0]
    fwd_list = []
    grad_list = []
    totals = None
    for k in range(TICKS):
        if k > 0:
            arriving = from_behind(fwd_list[-1], "section", 1)
            forward_x = jnp.where(section_pos == 0, new_batch[k - 1], arriving)
            coming = from_behind(grad_list[-1], "section", -1)
            cotangent = jnp.where(section_pos == last_section, loss_grad[k - 1], coming)
        unit_b, inverse_b, rows_b, picked_b, scale_b = backs[k]
        unit_f, _ = norm_of(forward_x)
        normed_f = (unit_f * gain_row).astype(bf16)
        gate_f = jax.nn.softplus(picked_of(normed_f, 0, k)) * live[0, k]
        lane = jnp.arange(LANES)
        extra = jnp.where(
            lane == 0,
            scale_b[:, None],
            jnp.where(lane == 1, own_totals[0], jnp.where(lane == 2, own_totals[1], 0.0)),
        ).astype(bf16)
        carried = jnp.concatenate([placed(1, k, cotangent), extra], axis=1)
        carried = carried.reshape(experts, capacity, width + LANES)
        grouped = (experts, capacity, width)
        got_f, got_b, got_carried = dispatch_rows(
            [placed(0, k, normed_f).reshape(grouped), rows_b.reshape(grouped), carried]
        )
        if totals is None:
            seen = got_carried[:, 0, width + 1 : width + 1 + TICKS].astype(f32)
            totals = jnp.sum(seen, axis=0)
        partial = expert_work(got_f, got_b, got_carried, gate_cols, up_cols, down_rows)
        halves = [
            jnp.sum(part.astype(f32).reshape(experts, 2, capacity, -1), axis=1).reshape(slots, -1)
            for part in collect_rows(partial)
        ]
        y_sum, dn_sum, dot_sum = halves
        combine_f = jnp.sum(table[0, k] * gate_f[:, :, None], axis=1)
        out_f = forward_x.astype(f32) + jnp.dot(
            combine_f, y_sum, precision=lax.Precision.HIGHEST
        )
        dots = jnp.sum(table[1, k] * dot_sum[:, 0], axis=-1)
        dpick = (dots + weight) * jax.nn.sigmoid(picked_b) * live[1, k]
        dlogit = jnp.sum(chosen[1, k] * dpick[:, :, None], axis=1)
        dnorm = jnp.dot(
            jnp.sum(table[1, k], axis=1),
            dn_sum,
            precision=lax.Precision.HIGHEST,
        ) + jnp.dot(dlogit, router_t, precision=lax.Precision.HIGHEST)
        scaled = dnorm * gain_row
        along = jnp.mean(scaled * unit_b, axis=-1, keepdims=True)
        grad_x = cotangent.astype(f32) + inverse_b * (scaled - unit_b * along)
        fwd_list.append(out_f.astype(bf16))
        grad_list.append(grad_x.astype(bf16))
        weight = weight * jnp.exp(4.0 * (totals[k] / share_total - 0.5))
    return (jnp.stack(fwd_list)[:, None], jnp.stack(grad_list)[:, None], weight.reshape(1))


def solution(mesh):
    in_specs = (
        P("section", "expert", None),
        P(None, "expert", None),
        P(None, "section", "expert", None),
        P("section", "expert", None),
        P(None, "expert", None),
        P(None, None, "section", "expert", None),
        P(None, None, "section", "expert"),
        P("section", None),
        P("section", None, None),
        P("section", None, "expert"),
        P("section", None, "expert"),
        P("section", "expert", None),
        P("section"),
    )
    out_specs = (
        P(None, "section", "expert", None),
        P(None, "section", "expert", None),
        P("section"),
    )
    return jax.shard_map(
        on_device, mesh=mesh, in_specs=in_specs, out_specs=out_specs, check_vma=False
    )
```

```python
import functools

import jax
import jax.numpy as jnp
from jax import lax
from jax.experimental import pallas as pl
from jax.experimental.pallas import tpu as pltpu
from jax.sharding import PartitionSpec as P

SPLIT = 4
TICKS = 2
LANES = 128


def from_behind(block, axis, distance):
    devices = range(lax.axis_size(axis))
    route = [(i - distance, i) for i in devices if i - distance in devices]
    return lax.ppermute(block, axis, route)


MESH = pl.DeviceIdType.MESH
SIDE = 4
CHIPS = SIDE * SIDE


class Place:
    def __init__(self):
        self.section = lax.axis_index("section")
        me = lax.axis_index("expert")
        self.chip = me // 2
        self.core = me % 2

    def away(self, step, sign):
        x = (self.chip // SIDE + sign * (step // SIDE) + SIDE) % SIDE
        y = (self.chip % SIDE + sign * (step % SIDE) + SIDE) % SIDE
        return x * SIDE + y

    def same_core(self, chip):
        return (self.section, chip * 2 + self.core)

    def other_core(self):
        return (self.section, self.chip * 2 + 1 - self.core)

    def greet(self):
        self.say()
        self.heard()

    def heard(self):
        pl.semaphore_wait(pltpu.get_barrier_semaphore(), CHIPS)

    def say(self):
        barrier = pltpu.get_barrier_semaphore()

        def signal(step, carry):
            pl.semaphore_signal(
                barrier,
                inc=1,
                device_id=self.same_core(self.away(step, 1)),
                device_id_type=MESH,
            )
            return carry

        lax.fori_loop(1, CHIPS, signal, 0)
        pl.semaphore_signal(
            barrier, inc=1, device_id=self.other_core(), device_id_type=MESH
        )


def steps_of(first, body):
    def step_once(step, carry):
        body(step)
        return carry

    lax.fori_loop(first, CHIPS, step_once, 0)


def remote(src, dst, send, recv, device):
    return pltpu.make_async_remote_copy(
        src_ref=src,
        dst_ref=dst,
        send_sem=send,
        recv_sem=recv,
        device_id=device,
        device_id_type=MESH,
    )


def dispatch_kernel(number, *refs):
    sources, results = refs[:number], refs[number : 2 * number]
    send, recv, pass_send, pass_recv, own = refs[2 * number :]
    at = Place()
    at.greet()
    streams = range(number)

    def outward(i, step):
        goal = at.away(step, 1)
        return remote(
            sources[i].at[goal // 2],
            results[i].at[at.core * CHIPS + at.chip],
            send.at[i, step],
            recv.at[i, step],
            at.same_core(goal),
        )

    def passed(i, step):
        slot = at.core * CHIPS + at.away(step, -1)
        return remote(
            results[i].at[slot],
            results[i].at[slot],
            pass_send.at[i, step],
            pass_recv.at[i, step],
            at.other_core(),
        )

    def own_copy(i):
        return pltpu.make_async_copy(
            sources[i].at[at.chip // 2], results[i].at[at.core * CHIPS + at.chip], own.at[i]
        )

    def start(step):
        for i in streams:
            outward(i, step).start()

    def hand_over(step):
        for i in streams:
            outward(i, step).wait_recv()
            passed(i, step).start()

    def finish(step):
        for i in streams:
            passed(i, step).wait_send()
            passed(i, step).wait_recv()

    def sent(step):
        for i in streams:
            outward(i, step).wait_send()

    for i in streams:
        own_copy(i).start()
    steps_of(1, start)
    for i in streams:
        own_copy(i).wait()
        passed(i, 0).start()
    steps_of(1, hand_over)
    steps_of(1, sent)
    steps_of(0, finish)


def times(left, right, right_dim):
    return lax.dot_general(
        left, right, (((1,), (right_dim,)), ((), ())), preferred_element_type=jnp.float32
    )


def work_kernel(*refs):
    rows_f, rows_b, carried, gate_ref, up_ref, down_ref = refs[:6]
    results, parts, arrived, joined = refs[6:9], refs[9:12], refs[12:15], refs[15:18]
    send, recv, pass_send, pass_recv = refs[18:]
    sources, capacity, width = rows_f.shape
    total_rows = sources * capacity
    f32, bf16 = jnp.float32, jnp.bfloat16
    at = Place()
    at.say()

    def passed(i, step):
        goal = at.away(step, 1)
        return remote(
            parts[i].at[(1 - at.core) * CHIPS + goal],
            arrived[i].at[goal],
            pass_send.at[i, step],
            pass_recv.at[i, step],
            at.other_core(),
        )

    def outward(i, step):
        goal = at.away(step, 1)
        return remote(
            joined[i].at[goal],
            results[i].at[at.chip],
            send.at[i, step],
            recv.at[i, step],
            at.same_core(goal),
        )

    def added(i, step):
        passed(i, step).wait_recv()
        goal = at.away(step, 1)
        total = parts[i][at.core * CHIPS + goal].astype(f32) + arrived[i][goal].astype(f32)
        return goal, total.astype(bf16)

    def send_all(streams):
        def send_on(step):
            for i in streams:
                goal, total = added(i, step)
                joined[i][goal] = total
                outward(i, step).start()

        steps_of(1, send_on)
        for i in streams:
            goal, total = added(i, 0)
            results[i][goal] = total

    def pass_all(streams):
        def start(step):
            for i in streams:
                passed(i, step).start()

        steps_of(1, start)
        for i in streams:
            passed(i, 0).start()

    def finish(step):
        for i in range(3):
            outward(i, step).wait_send()
            outward(i, step).wait_recv()

    def handed(step):
        for i in range(3):
            passed(i, step).wait_send()

    def flat(value):
        return value.astype(f32).reshape(total_rows, value.shape[-1]).astype(bf16)

    def first(rows):
        value = flat(rows[...])
        pre_gate = times(value, gate_ref[...], 0)
        pre_up = times(value, up_ref[...], 0)
        sigmoid_g = 1.0 / (1.0 + jnp.exp(-pre_gate))
        activated = pre_gate * sigmoid_g
        return pre_gate, pre_up, sigmoid_g, activated, (activated * pre_up).astype(bf16)

    chunk = min(width, 512)

    def store(i, at_col, value):
        shape = (sources, capacity, value.shape[-1])
        parts[i][:, :, at_col : at_col + value.shape[-1]] = value.reshape(shape).astype(bf16)

    hidden_f = first(rows_f)[-1]
    for col in range(0, width, chunk):
        store(0, col, times(hidden_f, down_ref[:, col : col + chunk], 0))
    at.heard()
    pass_all([0])
    pre_gate, pre_up, sigmoid_g, activated, hidden_b = first(rows_b)
    plain_h = times(flat(carried[:, :, :width]), down_ref[...], 1)
    send_all([0])
    scales = carried[:, :, width:].astype(f32).reshape(total_rows, LANES)[:, :1]
    inner_dot = jnp.sum(plain_h * hidden_b.astype(f32), axis=-1, keepdims=True)
    back_h = plain_h * scales
    d_gate = (back_h * pre_up * sigmoid_g * (1.0 + pre_gate * (1.0 - sigmoid_g))).astype(bf16)
    d_up = (back_h * activated).astype(bf16)
    for col in range(0, width, chunk):
        part = times(d_gate, gate_ref[col : col + chunk, :], 1)
        store(1, col, part + times(d_up, up_ref[col : col + chunk, :], 1))
    store(2, 0, jnp.broadcast_to(inner_dot, (total_rows, LANES)))
    pass_all([1, 2])
    send_all([1, 2])
    steps_of(0, handed)
    steps_of(1, finish)


def dispatch_rows(arrays):
    number = len(arrays)
    whole = pl.BlockSpec(memory_space=pltpu.VMEM)
    sems = pltpu.SemaphoreType.DMA
    return pl.pallas_call(
        functools.partial(dispatch_kernel, number),
        out_shape=[jax.ShapeDtypeStruct((2 * CHIPS,) + a.shape[1:], a.dtype) for a in arrays],
        in_specs=[whole] * number,
        out_specs=[whole] * number,
        scratch_shapes=[sems((number, CHIPS))] * 4 + [sems((number,))],
        compiler_params=pltpu.CompilerParams(
            collective_id=0, has_side_effects=True, vmem_limit_bytes=32 * 2**20
        ),
        name="dispatch_rows",
    )(*arrays)


def work_rows(rows_f, rows_b, carried, gate_q, up_q, down_q):
    capacity, width = rows_f.shape[1:]
    whole = pl.BlockSpec(memory_space=pltpu.VMEM)
    sems = pltpu.SemaphoreType.DMA
    tails = [(capacity, width), (capacity, width), (capacity, LANES)]

    def spaces(lead):
        return [pltpu.VMEM((lead,) + tail, jnp.bfloat16) for tail in tails]

    return pl.pallas_call(
        work_kernel,
        out_shape=[jax.ShapeDtypeStruct((CHIPS,) + tail, jnp.bfloat16) for tail in tails],
        in_specs=[whole] * 6,
        out_specs=[whole] * 3,
        scratch_shapes=spaces(2 * CHIPS) + spaces(CHIPS) * 2 + [sems((3, CHIPS))] * 4,
        compiler_params=pltpu.CompilerParams(
            collective_id=1, has_side_effects=True, vmem_limit_bytes=40 * 2**20
        ),
        name="work_rows",
    )(rows_f, rows_b, carried, gate_q, up_q, down_q)


def on_device(
    section_in,
    new_batch,
    stashed,
    grad_in,
    loss_grad,
    routes,
    counts,
    norm_gain,
    w_router,
    w_gate,
    w_up,
    w_down,
    lam,
):
    f32, bf16 = jnp.float32, jnp.bfloat16
    section_pos = lax.axis_index("section")
    last_section = lax.axis_size("section") - 1
    tok_rows, width = section_in.shape[1:]
    top_slots = routes.shape[-1]
    experts = w_router.shape[-1]
    capacity = SPLIT * min(
        tok_rows // (2 * SPLIT), 5 * tok_rows * top_slots // (4 * experts * SPLIT)
    )
    slots = experts * capacity
    entries = tok_rows * top_slots
    share_total = tok_rows * lax.axis_size("expert") * top_slots
    gain_row = norm_gain[0]
    router = w_router[0]
    router_t = router.astype(f32).T
    gate_cols, up_cols, down_rows = w_gate[0], w_up[0], w_down[0]
    route = routes[:, :, 0]
    count = counts[:, :, 0]
    flat = route.reshape(2, TICKS, entries)
    earlier = jnp.arange(entries)[None, :] < jnp.arange(entries)[:, None]
    rank = jnp.sum(
        ((flat[..., :, None] == flat[..., None, :]) & earlier).astype(jnp.int32), axis=-1
    )
    target = (flat * capacity + rank).reshape(2, TICKS, tok_rows, top_slots)
    live = jnp.arange(top_slots, dtype=jnp.int32) < count[..., None]
    table = ((target[..., None] == jnp.arange(slots)) & live[..., None]).astype(f32)
    chosen = (route[..., None] == jnp.arange(experts)).astype(f32)
    dispatch = jnp.sum(table, axis=3).astype(bf16)
    live = live.astype(f32)
    own_totals = jnp.sum(count[0], axis=-1).astype(f32)

    def norm_of(values):
        values = values.astype(f32)
        inverse = lax.rsqrt(jnp.mean(values * values, axis=-1, keepdims=True) + 1e-05)
        return values * inverse, inverse

    def picked_of(normed, m, k):
        logits = jnp.dot(normed, router, preferred_element_type=f32)
        return jnp.sum(chosen[m, k] * logits[:, None, :], axis=-1)

    def placed(m, k, rows):
        return lax.dot_general(
            dispatch[m, k], rows, (((0,), (0,)), ((), ())), preferred_element_type=f32
        ).astype(bf16)

    backs = []
    for k in range(TICKS):
        unit, inverse = norm_of(stashed[k, 0])
        normed = (unit * gain_row).astype(bf16)
        picked = picked_of(normed, 1, k)
        gate = jax.nn.softplus(picked) * live[1, k]
        scale = jnp.sum(table[1, k] * gate[:, :, None], axis=(0, 1))
        backs.append((unit, inverse, placed(1, k, normed), picked, scale))

    weight = lam[0]
    forward_x = section_in[0]
    cotangent = grad_in[0]
    fwd_list = []
    grad_list = []
    totals = None
    for k in range(TICKS):
        if k > 0:
            arriving = from_behind(fwd_list[-1], "section", 1)
            forward_x = jnp.where(section_pos == 0, new_batch[k - 1], arriving)
            coming = from_behind(grad_list[-1], "section", -1)
            cotangent = jnp.where(section_pos == last_section, loss_grad[k - 1], coming)
        unit_b, inverse_b, rows_b, picked_b, scale_b = backs[k]
        unit_f, _ = norm_of(forward_x)
        normed_f = (unit_f * gain_row).astype(bf16)
        gate_f = jax.nn.softplus(picked_of(normed_f, 0, k)) * live[0, k]
        lane = jnp.arange(LANES)
        extra = jnp.where(
            lane == 0,
            scale_b[:, None],
            jnp.where(lane == 1, own_totals[0], jnp.where(lane == 2, own_totals[1], 0.0)),
        ).astype(bf16)
        carried = jnp.concatenate([placed(1, k, cotangent), extra], axis=1)
        carried = carried.reshape(experts, capacity, width + LANES)
        grouped = (experts, capacity, width)
        got_f, got_b, got_carried = dispatch_rows(
            [placed(0, k, normed_f).reshape(grouped), rows_b.reshape(grouped), carried]
        )
        if totals is None:
            seen = got_carried[:, 0, width + 1 : width + 1 + TICKS].astype(f32)
            totals = jnp.sum(seen, axis=0)
        outputs = work_rows(got_f, got_b, got_carried, gate_cols, up_cols, down_rows)
        halves = [
            jnp.sum(part.astype(f32).reshape(experts, 2, capacity, -1), axis=1).reshape(slots, -1)
            for part in outputs
        ]
        y_sum, dn_sum, dot_sum = halves
        combine_f = jnp.sum(table[0, k] * gate_f[:, :, None], axis=1)
        out_f = forward_x.astype(f32) + jnp.dot(
            combine_f, y_sum, precision=lax.Precision.HIGHEST
        )
        dots = jnp.sum(table[1, k] * dot_sum[:, 0], axis=-1)
        dpick = (dots + weight) * jax.nn.sigmoid(picked_b) * live[1, k]
        dlogit = jnp.sum(chosen[1, k] * dpick[:, :, None], axis=1)
        dnorm = jnp.dot(
            jnp.sum(table[1, k], axis=1),
            dn_sum,
            precision=lax.Precision.HIGHEST,
        ) + jnp.dot(dlogit, router_t, precision=lax.Precision.HIGHEST)
        scaled = dnorm * gain_row
        along = jnp.mean(scaled * unit_b, axis=-1, keepdims=True)
        grad_x = cotangent.astype(f32) + inverse_b * (scaled - unit_b * along)
        fwd_list.append(out_f.astype(bf16))
        grad_list.append(grad_x.astype(bf16))
        weight = weight * jnp.exp(4.0 * (totals[k] / share_total - 0.5))
    return (jnp.stack(fwd_list)[:, None], jnp.stack(grad_list)[:, None], weight.reshape(1))


def solution(mesh):
    in_specs = (
        P("section", "expert", None),
        P(None, "expert", None),
        P(None, "section", "expert", None),
        P("section", "expert", None),
        P(None, "expert", None),
        P(None, None, "section", "expert", None),
        P(None, None, "section", "expert"),
        P("section", None),
        P("section", None, None),
        P("section", None, "expert"),
        P("section", None, "expert"),
        P("section", "expert", None),
        P("section"),
    )
    out_specs = (
        P(None, "section", "expert", None),
        P(None, "section", "expert", None),
        P("section"),
    )
    return jax.shard_map(
        on_device, mesh=mesh, in_specs=in_specs, out_specs=out_specs, check_vma=False
    )
```

```python
import functools

import jax
import jax.numpy as jnp
from jax import lax
from jax.experimental import pallas as pl
from jax.experimental.pallas import tpu as pltpu
from jax.sharding import PartitionSpec as P

SPLIT = 4
TICKS = 2
LANES = 128


def from_behind(block, axis, distance):
    devices = range(lax.axis_size(axis))
    route = [(i - distance, i) for i in devices if i - distance in devices]
    return lax.ppermute(block, axis, route)


MESH = pl.DeviceIdType.MESH
SIDE = 4
CHIPS = SIDE * SIDE


class Place:
    def __init__(self):
        self.section = lax.axis_index("section")
        me = lax.axis_index("expert")
        self.chip = me // 2
        self.core = me % 2

    def away(self, step, sign):
        x = (self.chip // SIDE + sign * (step // SIDE) + SIDE) % SIDE
        y = (self.chip % SIDE + sign * (step % SIDE) + SIDE) % SIDE
        return x * SIDE + y

    def same_core(self, chip):
        return (self.section, chip * 2 + self.core)

    def other_core(self):
        return (self.section, self.chip * 2 + 1 - self.core)

    def greet(self):
        self.say()
        self.heard()

    def heard(self):
        pl.semaphore_wait(pltpu.get_barrier_semaphore(), CHIPS)

    def say(self):
        barrier = pltpu.get_barrier_semaphore()

        def signal(step, carry):
            pl.semaphore_signal(
                barrier,
                inc=1,
                device_id=self.same_core(self.away(step, 1)),
                device_id_type=MESH,
            )
            return carry

        lax.fori_loop(1, CHIPS, signal, 0)
        pl.semaphore_signal(
            barrier, inc=1, device_id=self.other_core(), device_id_type=MESH
        )


def steps_of(first, body):
    def step_once(step, carry):
        body(step)
        return carry

    lax.fori_loop(first, CHIPS, step_once, 0)


def remote(src, dst, send, recv, device):
    return pltpu.make_async_remote_copy(
        src_ref=src,
        dst_ref=dst,
        send_sem=send,
        recv_sem=recv,
        device_id=device,
        device_id_type=MESH,
    )


def dispatch_kernel(*refs):
    move_f, move_b, given_f, given_b, given_g, extra = refs[:6]
    results, sources = refs[6:9], refs[9:12]
    send, recv, pass_send, pass_recv, own = refs[12:]
    at = Place()
    at.say()
    streams = range(3)
    experts, capacity, width = sources[0].shape
    for i, move, given in ((0, move_f, given_f), (1, move_b, given_b), (2, move_b, given_g)):
        placed = times(move[...], given[...], 0).reshape(experts, capacity, width)
        sources[i][:, :, :width] = placed.astype(jnp.bfloat16)
    tail = extra[...].reshape(experts, capacity, LANES)
    sources[2][:, :, width:] = tail.astype(jnp.bfloat16)
    at.heard()

    def outward(i, step):
        goal = at.away(step, 1)
        return remote(
            sources[i].at[goal // 2],
            results[i].at[at.core * CHIPS + at.chip],
            send.at[i, step],
            recv.at[i, step],
            at.same_core(goal),
        )

    def passed(i, step):
        slot = at.core * CHIPS + at.away(step, -1)
        return remote(
            results[i].at[slot],
            results[i].at[slot],
            pass_send.at[i, step],
            pass_recv.at[i, step],
            at.other_core(),
        )

    def own_copy(i):
        return pltpu.make_async_copy(
            sources[i].at[at.chip // 2], results[i].at[at.core * CHIPS + at.chip], own.at[i]
        )

    def start(step):
        for i in streams:
            outward(i, step).start()

    def hand_over(step):
        for i in streams:
            outward(i, step).wait_recv()
            passed(i, step).start()

    def finish(step):
        for i in streams:
            passed(i, step).wait_send()
            passed(i, step).wait_recv()

    def sent(step):
        for i in streams:
            outward(i, step).wait_send()

    for i in streams:
        own_copy(i).start()
    steps_of(1, start)
    for i in streams:
        own_copy(i).wait()
        passed(i, 0).start()
    steps_of(1, hand_over)
    steps_of(1, sent)
    steps_of(0, finish)


def times(left, right, right_dim):
    return lax.dot_general(
        left, right, (((1,), (right_dim,)), ((), ())), preferred_element_type=jnp.float32
    )


def work_kernel(*refs):
    rows_f, rows_b, carried, gate_ref, up_ref, down_ref = refs[:6]
    results, parts, arrived, joined = refs[6:9], refs[9:12], refs[12:15], refs[15:18]
    send, recv, pass_send, pass_recv = refs[18:]
    sources, capacity, width = rows_f.shape
    total_rows = sources * capacity
    f32, bf16 = jnp.float32, jnp.bfloat16
    at = Place()
    at.say()

    def passed(i, step):
        goal = at.away(step, 1)
        return remote(
            parts[i].at[(1 - at.core) * CHIPS + goal],
            arrived[i].at[goal],
            pass_send.at[i, step],
            pass_recv.at[i, step],
            at.other_core(),
        )

    def outward(i, step):
        goal = at.away(step, 1)
        return remote(
            joined[i].at[goal],
            results[i].at[at.chip],
            send.at[i, step],
            recv.at[i, step],
            at.same_core(goal),
        )

    def added(i, step):
        passed(i, step).wait_recv()
        goal = at.away(step, 1)
        total = parts[i][at.core * CHIPS + goal].astype(f32) + arrived[i][goal].astype(f32)
        return goal, total.astype(bf16)

    def send_all(streams):
        def send_on(step):
            for i in streams:
                goal, total = added(i, step)
                joined[i][goal] = total
                outward(i, step).start()

        steps_of(1, send_on)
        for i in streams:
            goal, total = added(i, 0)
            results[i][goal] = total

    def pass_all(streams):
        def start(step):
            for i in streams:
                passed(i, step).start()

        steps_of(1, start)
        for i in streams:
            passed(i, 0).start()

    def finish(step):
        for i in range(3):
            outward(i, step).wait_send()
            outward(i, step).wait_recv()

    def handed(step):
        for i in range(3):
            passed(i, step).wait_send()

    def flat(value):
        return value.astype(f32).reshape(total_rows, value.shape[-1]).astype(bf16)

    def first(rows):
        value = flat(rows[...])
        pre_gate = times(value, gate_ref[...], 0)
        pre_up = times(value, up_ref[...], 0)
        sigmoid_g = 1.0 / (1.0 + jnp.exp(-pre_gate))
        activated = pre_gate * sigmoid_g
        return pre_gate, pre_up, sigmoid_g, activated, (activated * pre_up).astype(bf16)

    chunk = min(width, 512)

    def store(i, at_col, value):
        shape = (sources, capacity, value.shape[-1])
        parts[i][:, :, at_col : at_col + value.shape[-1]] = value.reshape(shape).astype(bf16)

    hidden_f = first(rows_f)[-1]
    for col in range(0, width, chunk):
        store(0, col, times(hidden_f, down_ref[:, col : col + chunk], 0))
    at.heard()
    pass_all([0])
    pre_gate, pre_up, sigmoid_g, activated, hidden_b = first(rows_b)
    plain_h = times(flat(carried[:, :, :width]), down_ref[...], 1)
    send_all([0])
    scales = carried[:, :, width:].astype(f32).reshape(total_rows, LANES)[:, :1]
    inner_dot = jnp.sum(plain_h * hidden_b.astype(f32), axis=-1, keepdims=True)
    back_h = plain_h * scales
    d_gate = (back_h * pre_up * sigmoid_g * (1.0 + pre_gate * (1.0 - sigmoid_g))).astype(bf16)
    d_up = (back_h * activated).astype(bf16)
    for col in range(0, width, chunk):
        part = times(d_gate, gate_ref[col : col + chunk, :], 1)
        store(1, col, part + times(d_up, up_ref[col : col + chunk, :], 1))
    store(2, 0, jnp.broadcast_to(inner_dot, (total_rows, LANES)))
    pass_all([1, 2])
    send_all([1, 2])
    steps_of(0, handed)
    steps_of(1, finish)


def dispatch_rows(move_f, move_b, given_f, given_b, given_g, extra, experts):
    width = given_f.shape[1]
    capacity = move_f.shape[0] // experts
    whole = pl.BlockSpec(memory_space=pltpu.VMEM)
    sems = pltpu.SemaphoreType.DMA
    tails = [(capacity, width), (capacity, width), (capacity, width + LANES)]
    return pl.pallas_call(
        dispatch_kernel,
        out_shape=[jax.ShapeDtypeStruct((2 * CHIPS,) + t, jnp.bfloat16) for t in tails],
        in_specs=[whole] * 6,
        out_specs=[whole] * 3,
        scratch_shapes=[pltpu.VMEM((experts,) + t, jnp.bfloat16) for t in tails]
        + [sems((3, CHIPS))] * 4
        + [sems((3,))],
        compiler_params=pltpu.CompilerParams(
            collective_id=0, has_side_effects=True, vmem_limit_bytes=32 * 2**20
        ),
        name="dispatch_rows",
    )(move_f, move_b, given_f, given_b, given_g, extra)


def work_rows(rows_f, rows_b, carried, gate_q, up_q, down_q):
    capacity, width = rows_f.shape[1:]
    whole = pl.BlockSpec(memory_space=pltpu.VMEM)
    sems = pltpu.SemaphoreType.DMA
    tails = [(capacity, width), (capacity, width), (capacity, LANES)]

    def spaces(lead):
        return [pltpu.VMEM((lead,) + tail, jnp.bfloat16) for tail in tails]

    return pl.pallas_call(
        work_kernel,
        out_shape=[jax.ShapeDtypeStruct((CHIPS,) + tail, jnp.bfloat16) for tail in tails],
        in_specs=[whole] * 6,
        out_specs=[whole] * 3,
        scratch_shapes=spaces(2 * CHIPS) + spaces(CHIPS) * 2 + [sems((3, CHIPS))] * 4,
        compiler_params=pltpu.CompilerParams(
            collective_id=1, has_side_effects=True, vmem_limit_bytes=40 * 2**20
        ),
        name="work_rows",
    )(rows_f, rows_b, carried, gate_q, up_q, down_q)


def on_device(
    section_in,
    new_batch,
    stashed,
    grad_in,
    loss_grad,
    routes,
    counts,
    norm_gain,
    w_router,
    w_gate,
    w_up,
    w_down,
    lam,
):
    f32, bf16 = jnp.float32, jnp.bfloat16
    section_pos = lax.axis_index("section")
    last_section = lax.axis_size("section") - 1
    tok_rows, width = section_in.shape[1:]
    top_slots = routes.shape[-1]
    experts = w_router.shape[-1]
    capacity = SPLIT * min(
        tok_rows // (2 * SPLIT), 5 * tok_rows * top_slots // (4 * experts * SPLIT)
    )
    slots = experts * capacity
    entries = tok_rows * top_slots
    share_total = tok_rows * lax.axis_size("expert") * top_slots
    gain_row = norm_gain[0]
    router = w_router[0]
    router_t = router.astype(f32).T
    gate_cols, up_cols, down_rows = w_gate[0], w_up[0], w_down[0]
    route = routes[:, :, 0]
    count = counts[:, :, 0]
    flat = route.reshape(2, TICKS, entries)
    earlier = jnp.arange(entries)[None, :] < jnp.arange(entries)[:, None]
    rank = jnp.sum(
        ((flat[..., :, None] == flat[..., None, :]) & earlier).astype(jnp.int32), axis=-1
    )
    target = (flat * capacity + rank).reshape(2, TICKS, tok_rows, top_slots)
    live = jnp.arange(top_slots, dtype=jnp.int32) < count[..., None]
    table = ((target[..., None] == jnp.arange(slots)) & live[..., None]).astype(f32)
    chosen = (route[..., None] == jnp.arange(experts)).astype(f32)
    held = (target[:, :, None] == jnp.arange(slots)[:, None, None]) & live[:, :, None]
    moves = jnp.sum(held.astype(f32), axis=-1).astype(bf16)
    live = live.astype(f32)
    own_totals = jnp.sum(count[0], axis=-1).astype(f32)

    def norm_of(values):
        values = values.astype(f32)
        inverse = lax.rsqrt(jnp.mean(values * values, axis=-1, keepdims=True) + 1e-05)
        return values * inverse, inverse

    def picked_of(normed, m, k):
        logits = jnp.dot(normed, router, preferred_element_type=f32)
        return jnp.sum(chosen[m, k] * logits[:, None, :], axis=-1)

    backs = []
    for k in range(TICKS):
        unit, inverse = norm_of(stashed[k, 0])
        normed = (unit * gain_row).astype(bf16)
        picked = picked_of(normed, 1, k)
        gate = jax.nn.softplus(picked) * live[1, k]
        scale = jnp.sum(table[1, k] * gate[:, :, None], axis=(0, 1))
        backs.append((unit, inverse, normed, picked, scale))

    weight = lam[0]
    forward_x = section_in[0]
    cotangent = grad_in[0]
    fwd_list = []
    grad_list = []
    totals = None
    for k in range(TICKS):
        if k > 0:
            arriving = from_behind(fwd_list[-1], "section", 1)
            forward_x = jnp.where(section_pos == 0, new_batch[k - 1], arriving)
            coming = from_behind(grad_list[-1], "section", -1)
            cotangent = jnp.where(section_pos == last_section, loss_grad[k - 1], coming)
        unit_b, inverse_b, normed_b, picked_b, scale_b = backs[k]
        unit_f, _ = norm_of(forward_x)
        normed_f = (unit_f * gain_row).astype(bf16)
        gate_f = jax.nn.softplus(picked_of(normed_f, 0, k)) * live[0, k]
        lane = jnp.arange(LANES)
        extra = jnp.where(
            lane == 0,
            scale_b[:, None],
            jnp.where(lane == 1, own_totals[0], jnp.where(lane == 2, own_totals[1], 0.0)),
        )
        got_f, got_b, got_carried = dispatch_rows(
            moves[0, k], moves[1, k], normed_f, normed_b, cotangent, extra, experts
        )
        if totals is None:
            seen = got_carried[:, 0, width + 1 : width + 1 + TICKS].astype(f32)
            totals = jnp.sum(seen, axis=0)
        outputs = work_rows(got_f, got_b, got_carried, gate_cols, up_cols, down_rows)
        halves = [
            jnp.sum(part.astype(f32).reshape(experts, 2, capacity, -1), axis=1).reshape(slots, -1)
            for part in outputs
        ]
        y_sum, dn_sum, dot_sum = halves
        combine_f = jnp.sum(table[0, k] * gate_f[:, :, None], axis=1)
        out_f = forward_x.astype(f32) + jnp.dot(
            combine_f, y_sum, precision=lax.Precision.HIGHEST
        )
        dots = jnp.sum(table[1, k] * dot_sum[:, 0], axis=-1)
        dpick = (dots + weight) * jax.nn.sigmoid(picked_b) * live[1, k]
        dlogit = jnp.sum(chosen[1, k] * dpick[:, :, None], axis=1)
        dnorm = jnp.dot(
            jnp.sum(table[1, k], axis=1),
            dn_sum,
            precision=lax.Precision.HIGHEST,
        ) + jnp.dot(dlogit, router_t, precision=lax.Precision.HIGHEST)
        scaled = dnorm * gain_row
        along = jnp.mean(scaled * unit_b, axis=-1, keepdims=True)
        grad_x = cotangent.astype(f32) + inverse_b * (scaled - unit_b * along)
        fwd_list.append(out_f.astype(bf16))
        grad_list.append(grad_x.astype(bf16))
        weight = weight * jnp.exp(4.0 * (totals[k] / share_total - 0.5))
    return (jnp.stack(fwd_list)[:, None], jnp.stack(grad_list)[:, None], weight.reshape(1))


def solution(mesh):
    in_specs = (
        P("section", "expert", None),
        P(None, "expert", None),
        P(None, "section", "expert", None),
        P("section", "expert", None),
        P(None, "expert", None),
        P(None, None, "section", "expert", None),
        P(None, None, "section", "expert"),
        P("section", None),
        P("section", None, None),
        P("section", None, "expert"),
        P("section", None, "expert"),
        P("section", "expert", None),
        P("section"),
    )
    out_specs = (
        P(None, "section", "expert", None),
        P(None, "section", "expert", None),
        P("section"),
    )
    return jax.shard_map(
        on_device, mesh=mesh, in_specs=in_specs, out_specs=out_specs, check_vma=False
    )
```
